128 devices in a mesh: row: 16 (over y_hi, z, core), col: 8 (over x, y_lo).
Axes of the slice: x: 4, y: 4 (y_hi: 2, y_lo: 2; y = y_hi * 2 + y_lo), z: 4, core: 2. Of those that a mesh axis runs over, the one named last changes fastest.
Arguments:
- query: bfloat16 [384, 1024, 128], P('row', 'col'), may hold values from -12 to 12
- key: bfloat16 [384, 1024, 128], P('row', 'col'), may hold values from -6 to 6
- value: bfloat16 [384, 1024, 128], P('row', 'col'), may hold values from -6 to 6
- gate: bfloat16 [384, 1024, 128], P('row', 'col'), may hold values from -6 to 6
- d_out: bfloat16 [384, 1024, 128], P('row', 'col'), may hold values from -6 to 6
- bias: bfloat16 [4, 1024, 1024], P(None, 'col'), may hold values from -6 to 6
- length: int32 [1], replicated, may hold values from 513 to 1024
Outputs:
- d_query: bfloat16 [384, 1024, 128], P('row', 'col')
- d_key: bfloat16 [384, 1024, 128], P('row', 'col')
- d_value: bfloat16 [384, 1024, 128], P('row', 'col')
- d_gate: bfloat16 [384, 1024, 128], P('row', 'col')
- d_bias: float32 [4, 1024, 1024], P(None, 'row', 'col')
The draws below stay inside these ranges and needn't reach their ends.
All inputs are finite; a program needn't handle non-finite values.
Results may differ from the reference program's by a relative error of at most 0.014.
Values may be sent and summed in bfloat16 or wider, within the bound.
A program may use at most 128 MiB of HBM per device.

```python
import jax
import jax.numpy as jnp
from jax import lax

N = 1024
HEADS = 4
HEAD_DIM = 32
GROUP = 4
HH = 128
NI = 384
BLK = 128
N_COL = 8


def draw_key(key, part):
    base = jax.random.normal(jax.random.fold_in(key, 11), (NI, N, HEADS * HEAD_DIM), jnp.float32)
    base = jnp.clip(base, -6.0, 6.0)
    return base.astype(jnp.bfloat16)


def draw_query(key, part):
    base = jax.random.normal(jax.random.fold_in(key, 13), (NI, N, HEADS * HEAD_DIM), jnp.float32)
    base = jnp.clip(base, -6.0, 6.0)
    return base.astype(jnp.bfloat16)


def shard_levels(key, extent, shards, least, top_value):
    loudness = 1.0
    for position, shards_of in shards:
        draws = jax.random.uniform(jax.random.fold_in(jax.random.fold_in(key, 6), position), (shards_of,), jnp.float32, least / len(shards), top_value / len(shards))
        loudness = loudness * jnp.repeat(jnp.exp(draws), extent[position] // shards_of).reshape((-1,) + (1,) * (len(extent) - 1 - position))
    return loudness


def bell_draw(stream_key, dims, width, bound, cuts=(), held_as=jnp.bfloat16):
    drawn = jax.random.normal(stream_key, dims, jnp.float32) * width
    if len(cuts) > 0:
        drawn = shard_levels(stream_key, dims, cuts, -0.22, 0.18) * drawn
    return jnp.clip(drawn, min=-bound, max=bound).astype(held_as)


def setup_inputs(seed: int = 0) -> dict:
    seeds = jax.random.split(jax.random.key(seed), 8)
    return {
        "query": draw_query(jax.random.fold_in(seeds[7], 71), 0),
        "key": draw_key(jax.random.fold_in(seeds[7], 71), 0),
        "value": bell_draw(seeds[2], (NI, N, HH), 1.0, 6.0, ((0, 16), (1, 8))),
        "gate": bell_draw(seeds[3], (NI, N, HH), 1.0, 6.0, ((0, 16), (1, 8))),
        "d_out": bell_draw(seeds[4], (NI, N, HH), 1.0, 6.0, ((0, 16), (1, 8))),
        "bias": bell_draw(seeds[5], (HEADS, N, N), 1.0, 6.0, ((1, 8),)),
        "length": jax.random.randint(seeds[6], (1,), N // 2 + 1, N + 1).astype(jnp.int32),
    }


def reference(query, key, value, gate, d_out, bias, length):
    scaling = HEAD_DIM ** -0.5
    key_valid = jnp.arange(N) < length[0]
    bias_f = bias.astype(jnp.float32)
    blocks = NI // GROUP

    def split(array):
        return array.reshape(blocks, GROUP, N, HEADS * HEAD_DIM)

    def one_block(bias_sum, pieces):
        query_block, key_block, value_block, gate_block, dout_block = pieces
        q_heads = query_block.astype(jnp.float32).reshape(GROUP, N, HEADS, HEAD_DIM)
        k_heads = key_block.astype(jnp.float32).reshape(GROUP, N, HEADS, HEAD_DIM)
        v_heads = value_block.astype(jnp.float32).reshape(GROUP, N, HEADS, HEAD_DIM)
        logits = jnp.einsum("ijhc,ikhc->ihjk", q_heads, k_heads) * scaling + bias_f[None]
        logits = jnp.where(key_valid, logits, -1e30)
        row_max = jnp.max(logits, axis=-1, keepdims=True)
        exponent = jnp.where(key_valid, jnp.exp(logits - row_max), 0.0)
        weights = exponent / jnp.sum(exponent, axis=-1, keepdims=True)
        weights_bf = weights.astype(jnp.bfloat16).astype(jnp.float32)
        attended = jnp.einsum("ihjk,ikhc->ijhc", weights_bf, v_heads)
        gate_sig = jax.nn.sigmoid(gate_block.astype(jnp.float32).reshape(GROUP, N, HEADS, HEAD_DIM))
        upstream = dout_block.astype(jnp.float32).reshape(GROUP, N, HEADS, HEAD_DIM)
        gate_grad = (upstream * attended * gate_sig * (1.0 - gate_sig)).astype(jnp.bfloat16)
        grad_att = upstream * gate_sig
        row_dot = jnp.sum(grad_att * attended, axis=-1)
        grad_att_bf = grad_att.astype(jnp.bfloat16).astype(jnp.float32)
        grad_weight = jnp.einsum("ijhc,ikhc->ihjk", grad_att_bf, v_heads)
        grad_logits = weights * (grad_weight - jnp.transpose(row_dot, (0, 2, 1))[..., None])
        grad_logits_bf = grad_logits.astype(jnp.bfloat16).astype(jnp.float32)
        query_grad = (jnp.einsum("ihjk,ikhc->ijhc", grad_logits_bf, k_heads) * scaling).astype(jnp.bfloat16)
        grad_split = grad_logits_bf.reshape(GROUP, HEADS, N_COL, BLK, N)
        weight_split = weights_bf.reshape(GROUP, HEADS, N_COL, BLK, N)
        query_split = q_heads.reshape(GROUP, N_COL, BLK, HEADS, HEAD_DIM)
        att_split = grad_att_bf.reshape(GROUP, N_COL, BLK, HEADS, HEAD_DIM)
        key_parts = (jnp.einsum("ihnjk,injhc->nikhc", grad_split, query_split) * scaling).astype(jnp.bfloat16)
        key_parts = lax.optimization_barrier(key_parts)
        key_grad = jnp.sum(key_parts.astype(jnp.float32), axis=0).astype(jnp.bfloat16)
        value_parts = jnp.einsum("ihnjk,injhc->nikhc", weight_split, att_split).astype(jnp.bfloat16)
        value_parts = lax.optimization_barrier(value_parts)
        value_grad = jnp.sum(value_parts.astype(jnp.float32), axis=0).astype(jnp.bfloat16)
        shaped = (GROUP, N, HEADS * HEAD_DIM)
        outputs = (query_grad.reshape(shaped), key_grad.reshape(shaped), value_grad.reshape(shaped), gate_grad.reshape(shaped))
        return bias_sum + jnp.sum(grad_logits, axis=0), outputs

    start = jnp.zeros((HEADS, N, N), jnp.float32)
    bias_grad, stacked = lax.scan(one_block, start, (split(query), split(key), split(value), split(gate), split(d_out)))
    whole = (NI, N, HEADS * HEAD_DIM)
    return (stacked[0].reshape(whole), stacked[1].reshape(whole), stacked[2].reshape(whole), stacked[3].reshape(whole), bias_grad)
```

```python
import functools
import math

import jax
import jax.numpy as jnp
from jax import lax
from jax.experimental import pallas as pl
from jax.experimental.pallas import tpu as pltpu
from jax.sharding import PartitionSpec as P

MESH = pl.DeviceIdType.MESH
BF = jnp.bfloat16
F32 = jnp.float32
HEADS = 4
C = 32
SCALE = C**-0.5
LOG2E = math.log2(math.e)
CI = 2
KC = 256
NN = (((1,), (0,)), ((), ()))
NT = (((1,), (1,)), ((), ()))


def dot(a, b, dims=NN):
    return lax.dot_general(a, b, dims, preferred_element_type=F32)


def sigmoid(x):
    return 1.0 / (1.0 + jnp.exp(-x))


def compute_row(qt, gat, kt, vt, bt_ref, d_ref, s_ref, e_ref, ds_ref, k2_ref, v1_ref):
    n = kt.shape[1]
    width = qt.shape[1]
    k2_ref[...] = jnp.concatenate([kt, kt], axis=0).T
    v1t = jnp.concatenate([vt, jnp.ones((16, n), BF)], axis=0)
    v1_ref[...] = v1t.T
    row = lax.broadcasted_iota(jnp.int32, (16, width), 0)
    q = qt.astype(F32) * (SCALE * LOG2E)
    q_hi = q.astype(BF)
    q_lo = (q - q_hi.astype(F32)).astype(BF)
    q2 = jnp.concatenate([q_hi, q_lo], axis=0)
    peak = None
    for c in range(n // KC):
        ks = slice(c * KC, (c + 1) * KC)
        s = dot(k2_ref[ks, :], q2) + bt_ref[ks, :]
        s_ref[ks, :] = s
        part = jnp.max(s.reshape(KC // 8, 8, width), axis=0)
        peak = part if peak is None else jnp.maximum(peak, part)
    peak = jnp.max(peak, axis=0, keepdims=True)
    for c in range(n // KC):
        ks = slice(c * KC, (c + 1) * KC)
        e = jnp.exp2(s_ref[ks, :] - peak)
        s_ref[ks, :] = e
        e_ref[ks, :] = e.astype(BF)
    summed = dot(v1t, e_ref[...])
    inv = 1.0 / summed[C : C + 1, :]
    att = summed[:C, :] * inv
    ga = gat.astype(F32)
    row_dot = jnp.sum(ga * att, axis=0, keepdims=True) * inv
    ga_n = (ga * inv).astype(BF)
    r_hi = row_dot.astype(BF).astype(F32)
    r_lo = row_dot - r_hi
    ext = jnp.where(row == 0, -r_hi, jnp.where(row == 1, -r_lo, 0.0)).astype(BF)
    g1 = jnp.concatenate([ga_n, ext], axis=0)
    for c in range(n // KC):
        ks = slice(c * KC, (c + 1) * KC)
        ds = dot(v1_ref[ks, :], g1) * s_ref[ks, :]
        d_ref[ks, :] += ds
        ds_ref[ks, :] = ds.astype(BF)
    dq = dot(kt, ds_ref[...]) * SCALE
    dk = dot(qt, ds_ref[...], NT) * SCALE
    dv = dot(ga_n, e_ref[...], NT)
    return dq, att, dk, dv


def kernel(
    q, k, v, g, do, bias, length,
    dq, dk, dv, dg, db,
    snd, rx, ry, dkv, ryd, outs, fin,
    bts, btr, bt, dacc, s_ref, e_ref, ds_ref, k2_ref, v1_ref,
    dt, t1s, t1r, t2s, t2u, t3r, t4s, t4r,
    s1, r1, s2, r2, s4, r4, s5, r5, sb, rb, st, rt,
):
    r, c = lax.axis_index("row"), lax.axis_index("col")
    yh, z, core = lax.div(r, 8), lax.rem(lax.div(r, 2), 4), lax.rem(r, 2)
    x, yl = lax.div(c, 2), lax.rem(c, 2)
    rows = q.shape[0]
    chunks = rows // CI
    xs = [lax.rem(x + d, 4) for d in (1, 2, 3)]
    x_ids = [(r, t * 2 + yl) for t in xs]
    y_id = (r, x * 2 + 1 - yl)
    core_id = (r + 1 - 2 * core, c)
    peers = []
    for dyh in (0, 1):
        for dz in range(4):
            if dyh or dz:
                yh2 = yh if dyh == 0 else 1 - yh
                peers.append((yh2, lax.rem(z + dz, 4)))
    peer_ids = [(a * 8 + b * 2 + core, c) for a, b in peers]

    everyone = x_ids + [y_id, core_id] + peer_ids
    barrier = pltpu.get_barrier_semaphore()
    for one in everyone:
        pl.semaphore_signal(barrier, inc=1, device_id=one, device_id_type=MESH)

    def copy(src, dst, send, recv, to):
        return pltpu.make_async_remote_copy(
            src_ref=src, dst_ref=dst, send_sem=send, recv_sem=recv, device_id=to, device_id_type=MESH
        )

    def in_copy(n, d):
        i = pl.ds(n * CI, CI)
        return copy(snd.at[i, xs[d]], rx.at[i, x], s1.at[n, d], r1.at[n, d], x_ids[d])

    def y_copy(n):
        i = pl.ds(n * CI, CI)
        return copy(rx.at[i, :, pl.ds(2, 2)], ry.at[i], s2.at[n], r2.at[n], y_id)

    def back_copy(n):
        i = pl.ds(n * CI, CI)
        return copy(dkv.at[i, 1], ryd.at[i], s4.at[n], r4.at[n], y_id)

    def out_copy(n, d):
        i = pl.ds(n * CI, CI)
        return copy(outs.at[i, xs[d]], fin.at[i, x], s5.at[n, d], r5.at[n, d], x_ids[d])

    def bias_copy(d):
        return copy(bts.at[xs[d]], btr.at[x], sb.at[d], rb.at[d], x_ids[d])

    def prepare(n):
        for one in range(CI):
            i = n * CI + one
            ga = do[i].astype(F32) * sigmoid(g[i].astype(F32))
            for t, array in enumerate((q[i], ga.astype(BF), k[i], v[i])):
                snd[i, :, t] = array.T.reshape(HEADS, C, 128)
            rx[i, x] = snd[i, x]

    prepare(0)
    pl.semaphore_wait(barrier, len(everyone))
    for d in range(3):
        in_copy(0, d).start()

    def bias_head(h, _):
        for p in range(2):
            for b in range(4):
                at = pl.multiple_of((2 * b + (yl if p == 0 else 1 - yl)) * 128, 128)
                bts[h, pl.ds((p * 4 + b) * 128, 128), :] = bias[h, :, pl.ds(at, 128)].T
        return 0

    lax.fori_loop(0, HEADS, bias_head, 0)
    for d in range(3):
        bias_copy(d).start()
    btr[x] = bts[x]

    def prepare_and_send(n, _):
        prepare(n)
        for d in range(3):
            in_copy(n, d).start()
        return 0

    lax.fori_loop(1, chunks, prepare_and_send, 0)

    dacc[...] = jnp.zeros_like(dacc)
    for d in range(3):
        in_copy(0, d).wait_recv()
    y_copy(0).start()
    for d in range(3):
        bias_copy(d).wait_recv()
    valid = length[0]
    for p in range(2):
        for b in range(4):
            first = (2 * b + (yl if p == 0 else 1 - yl)) * 128
            ks = pl.ds((p * 4 + b) * 128, 128)
            live = lax.broadcasted_iota(jnp.int32, (128, 128), 0) + first < valid
            for t in range(4):
                bt[ks, pl.ds(t * 128, 128)] = jnp.where(live, btr[t, ks, :].astype(F32) * LOG2E, -1e30)

    def compute(n):
        def one(j, _):
            i = n * CI + j
            qt = jnp.concatenate([rx[i, t, 0] for t in range(4)], axis=1)
            gat = jnp.concatenate([rx[i, t, 1] for t in range(4)], axis=1)
            kt = jnp.concatenate([rx[i, t, 2] for t in range(4)] + [ry[i, t, 0] for t in range(4)], axis=1)
            vt = jnp.concatenate([rx[i, t, 3] for t in range(4)] + [ry[i, t, 1] for t in range(4)], axis=1)
            a, b, e, f = compute_row(qt, gat, kt, vt, bt, dacc, s_ref, e_ref, ds_ref, k2_ref, v1_ref)
            for t in range(4):
                js = slice(t * 128, t * 128 + 128)
                outs[i, t, 0] = a[:, js].astype(BF)
                outs[i, t, 1] = b[:, js].astype(BF)
                for p in range(2):
                    ks = slice((p * 4 + t) * 128, (p * 4 + t) * 128 + 128)
                    dkv[i, p, t, 0] = e[:, ks].astype(BF)
                    dkv[i, p, t, 1] = f[:, ks].astype(BF)
            return 0

        lax.fori_loop(0, CI, one, 0)

    def add_and_send(n):
        back_copy(n).wait_recv()
        for one in range(CI):
            i = n * CI + one
            total = dkv[i, 0].astype(F32) + ryd[i].astype(F32)
            outs[i, :, pl.ds(2, 2)] = total.astype(BF)
            fin[i, x] = outs[i, x]
        for d in range(3):
            out_copy(n, d).start()

    def finish(n):
        for d in range(3):
            out_copy(n, d).wait_recv()
        for one in range(CI):
            i = n * CI + one
            dq[i] = fin[i, :, 0].reshape(128, 128).T
            dk[i] = fin[i, :, 2].reshape(128, 128).T
            dv[i] = fin[i, :, 3].reshape(128, 128).T
            att = fin[i, :, 1].reshape(128, 128).T.astype(F32)
            s = sigmoid(g[i].astype(F32))
            dg[i] = (do[i].astype(F32) * att * s * (1.0 - s)).astype(BF)

    def step(n, _):
        @pl.when(n + 1 < chunks)
        def _():
            for d in range(3):
                in_copy(n + 1, d).wait_recv()
            y_copy(n + 1).start()

        y_copy(n).wait_recv()
        compute(n)
        back_copy(n).start()

        @pl.when(n >= 1)
        def _():
            add_and_send(n - 1)

        @pl.when(n >= 2)
        def _():
            finish(n - 2)

        return 0

    lax.fori_loop(0, chunks, step, 0)

    for t in range(4):
        for b in range(8):
            dt[pl.ds(t * 128, 128), pl.ds(b * 128, 128)] = dacc[pl.ds(b * 128, 128), pl.ds(t * 128, 128)].T
    for t in range(4):
        t1s[t] = dt[pl.ds(pl.multiple_of(t * 128 + 64 * (1 - core), 64), 64), :].astype(BF)
    one = copy(t1s, t1r, st.at[0], rt.at[0], core_id)
    one.start()
    add_and_send(chunks - 1)
    one.wait_recv()
    for t in range(4):
        total = dt[pl.ds(pl.multiple_of(t * 128 + 64 * core, 64), 64), :] + t1r[t].astype(F32)
        t2u[yl, t] = total[:, :512].astype(BF)
        t2s[t] = total[:, 512:].astype(BF)
    two = copy(t2s, t2u.at[yl], st.at[1], rt.at[1], y_id)
    two.start()
    finish(chunks - 2)
    two.wait_recv()
    me = yh * 4 + z
    three = []
    for d, (a, b) in enumerate(peers):
        src = t2u.at[lax.rem(b, 2), 2 * a + lax.div(b, 2)]
        three.append(copy(src, t3r.at[me], st.at[2 + d], rt.at[2 + d], peer_ids[d]))
        three[-1].start()
    t3r[me] = t2u[lax.rem(z, 2), 2 * yh + lax.div(z, 2)]
    finish(chunks - 1)
    for one_copy in three:
        one_copy.wait_recv()
    total = t3r[0].astype(F32)
    for s in range(1, 8):
        total += t3r[s].astype(F32)
    for t in range(4):
        t4s[t] = total[:, t * 128 : t * 128 + 128].astype(BF)
    four = []
    for d in range(3):
        four.append(copy(t4s.at[xs[d]], t4r.at[x], st.at[9 + d], rt.at[9 + d], x_ids[d]))
        four[-1].start()
    t4r[x] = t4s[x]
    for one_copy in four:
        one_copy.wait_recv()
    for h in range(HEADS):
        db[h] = t4r[h].astype(F32)

    def drain(n, _):
        for d in range(3):
            in_copy(n, d).wait_send()
            out_copy(n, d).wait_send()
        y_copy(n).wait_send()
        back_copy(n).wait_send()
        return 0

    lax.fori_loop(0, chunks, drain, 0)
    for d in range(3):
        bias_copy(d).wait_send()
    for one_copy in [one, two] + three + four:
        one_copy.wait_send()


def on_device(query, key, value, gate, d_out, bias, length):
    rows = query.shape[0]
    chunks = rows // CI
    vmem = pl.BlockSpec(memory_space=pltpu.VMEM)
    pair = jax.ShapeDtypeStruct(query.shape, BF)
    dma = pltpu.SemaphoreType.DMA
    out = pl.pallas_call(
        kernel,
        out_shape=[pair, pair, pair, pair, jax.ShapeDtypeStruct((HEADS, 64, 128), F32)],
        in_specs=[vmem] * 6 + [pl.BlockSpec(memory_space=pltpu.SMEM)],
        out_specs=[vmem] * 5,
        scratch_shapes=[
            pltpu.VMEM((rows, 4, 4, C, 128), BF),
            pltpu.VMEM((rows, 4, 4, C, 128), BF),
            pltpu.VMEM((rows, 4, 2, C, 128), BF),
            pltpu.VMEM((rows, 2, 4, 2, C, 128), BF),
            pltpu.VMEM((rows, 4, 2, C, 128), BF),
            pltpu.VMEM((rows, 4, 4, C, 128), BF),
            pltpu.VMEM((rows, 4, 4, C, 128), BF),
            pltpu.VMEM((4, 1024, 128), BF),
            pltpu.VMEM((4, 1024, 128), BF),
            pltpu.VMEM((1024, 512), F32),
            pltpu.VMEM((1024, 512), F32),
            pltpu.VMEM((1024, 512), F32),
            pltpu.VMEM((1024, 512), BF),
            pltpu.VMEM((1024, 512), BF),
            pltpu.VMEM((1024, 64), BF),
            pltpu.VMEM((1024, 48), BF),
            pltpu.VMEM((512, 1024), F32),
            pltpu.VMEM((4, 64, 1024), BF),
            pltpu.VMEM((4, 64, 1024), BF),
            pltpu.VMEM((4, 64, 512), BF),
            pltpu.VMEM((2, 4, 64, 512), BF),
            pltpu.VMEM((8, 64, 512), BF),
            pltpu.VMEM((4, 64, 128), BF),
            pltpu.VMEM((4, 64, 128), BF),
            dma((chunks, 3)), dma((chunks, 3)),
            dma((chunks,)), dma((chunks,)),
            dma((chunks,)), dma((chunks,)),
            dma((chunks, 3)), dma((chunks, 3)),
            dma((3,)), dma((3,)),
            dma((12,)), dma((12,)),
        ],
        compiler_params=pltpu.CompilerParams(
            collective_id=0, has_side_effects=True, vmem_limit_bytes=60 * 2**20
        ),
    )(query, key, value, gate, d_out, bias, length)
    return tuple(out)


def solution(mesh):
    pair = P("row", "col", None)
    return jax.shard_map(
        on_device,
        mesh=mesh,
        in_specs=(pair,) * 5 + (P(None, "col", None), P()),
        out_specs=(pair,) * 4 + (P(None, "row", "col"),),
        check_vma=False,
    )
```

```python
import functools
import math

import jax
import jax.numpy as jnp
from jax import lax
from jax.experimental import pallas as pl
from jax.experimental.pallas import tpu as pltpu
from jax.sharding import PartitionSpec as P

MESH = pl.DeviceIdType.MESH
BF = jnp.bfloat16
F32 = jnp.float32
HEADS = 4
C = 32
SCALE = C**-0.5
LOG2E = math.log2(math.e)
CI = 2
LAG = 8
ADD = 2
KC = 256
NN = (((1,), (0,)), ((), ()))
NT = (((1,), (1,)), ((), ()))


def dot(a, b, dims=NN):
    return lax.dot_general(a, b, dims, preferred_element_type=F32)


def sigmoid(x):
    return 1.0 / (1.0 + jnp.exp(-x))


def compute_row(qt, gat, kt, vt, bt_ref, d_ref, s_ref, e_ref, ds_ref, k2_ref, v1_ref):
    n = kt.shape[1]
    width = qt.shape[1]
    k2_ref[...] = jnp.concatenate([kt, kt], axis=0).T
    v1t = jnp.concatenate([vt, jnp.ones((16, n), BF)], axis=0)
    v1_ref[...] = v1t.T
    row = lax.broadcasted_iota(jnp.int32, (16, width), 0)
    q = qt.astype(F32) * (SCALE * LOG2E)
    q_hi = q.astype(BF)
    q_lo = (q - q_hi.astype(F32)).astype(BF)
    q2 = jnp.concatenate([q_hi, q_lo], axis=0)
    peak = None
    for c in range(n // KC):
        ks = slice(c * KC, (c + 1) * KC)
        s = dot(k2_ref[ks, :], q2) + bt_ref[ks, :]
        s_ref[ks, :] = s
        part = jnp.max(s.reshape(KC // 8, 8, width), axis=0)
        peak = part if peak is None else jnp.maximum(peak, part)
    peak = jnp.max(peak, axis=0, keepdims=True)
    for c in range(n // KC):
        ks = slice(c * KC, (c + 1) * KC)
        e = jnp.exp2(s_ref[ks, :] - peak)
        s_ref[ks, :] = e
        e_ref[ks, :] = e.astype(BF)
    summed = dot(v1t, e_ref[...])
    inv = 1.0 / summed[C : C + 1, :]
    att = summed[:C, :] * inv
    ga = gat.astype(F32)
    row_dot = jnp.sum(ga * att, axis=0, keepdims=True) * inv
    ga_n = (ga * inv).astype(BF)
    r_hi = row_dot.astype(BF).astype(F32)
    r_lo = row_dot - r_hi
    ext = jnp.where(row == 0, -r_hi, jnp.where(row == 1, -r_lo, 0.0)).astype(BF)
    g1 = jnp.concatenate([ga_n, ext], axis=0)
    for c in range(n // KC):
        ks = slice(c * KC, (c + 1) * KC)
        ds = dot(v1_ref[ks, :], g1) * s_ref[ks, :]
        d_ref[ks, :] += ds
        ds_ref[ks, :] = ds.astype(BF)
    dq = dot(kt, ds_ref[...]) * SCALE
    dk = dot(qt, ds_ref[...], NT) * SCALE
    dv = dot(ga_n, e_ref[...], NT)
    return dq, att, dk, dv


def kernel(
    q_hbm, k_hbm, v_hbm, g_hbm, do_hbm, bias_hbm, length,
    dq, dk, dv, dg, db,
    q, k, v, g, do, bias, sl,
    snd, rx, ry, dkv, ryd, outs, fin,
    bts, btr, bt, dacc, s_ref, e_ref, ds_ref, k2_ref, v1_ref,
    dt, t1s, t1r, t2s, t3r, t4s, t4r,
    s1, r1, s2, r2, s4, r4, s5, r5, sb, rb, st, rt,
):
    loads = []
    for part, i in enumerate((pl.ds(0, CI), pl.ds(CI, q.shape[0] - CI))):
        for t, (far, near) in enumerate(((g_hbm, g), (do_hbm, do), (q_hbm, q), (k_hbm, k), (v_hbm, v))):
            loads.append(pltpu.make_async_copy(far.at[i], near.at[i], sl.at[part * 6 + t]))
        if part == 0:
            loads.append(pltpu.make_async_copy(bias_hbm, bias, sl.at[5]))
    for one_load in loads:
        one_load.start()

    r, c = lax.axis_index("row"), lax.axis_index("col")
    yh, z, core = lax.div(r, 8), lax.rem(lax.div(r, 2), 4), lax.rem(r, 2)
    x, yl = lax.div(c, 2), lax.rem(c, 2)
    rows = q.shape[0]
    chunks = rows // CI
    xs = [lax.rem(x + d, 4) for d in (1, 2, 3)]
    x_ids = [(r, t * 2 + yl) for t in xs]
    y_id = (r, x * 2 + 1 - yl)
    core_id = (r + 1 - 2 * core, c)
    peers = []
    for dyh in (0, 1):
        for dz in range(4):
            if dyh or dz:
                yh2 = yh if dyh == 0 else 1 - yh
                peers.append((yh2, lax.rem(z + dz, 4)))
    peer_ids = [(a * 8 + b * 2 + core, c) for a, b in peers]

    swap_row = yh * 8 + (lax.div(z, 2) * 2 + yl) * 2 + core
    swap_yl = lax.rem(z, 2)
    swaps = swap_yl != yl
    last_ids = [(swap_row, t * 2 + swap_yl) for t in xs]
    twin_id = (swap_row, x * 2 + swap_yl)

    everyone = x_ids + [y_id, core_id] + peer_ids + last_ids
    barrier = pltpu.get_barrier_semaphore()
    for one in everyone:
        pl.semaphore_signal(barrier, inc=1, device_id=one, device_id_type=MESH)

    @pl.when(swaps)
    def _():
        pl.semaphore_signal(barrier, inc=1, device_id=twin_id, device_id_type=MESH)

    def copy(src, dst, send, recv, to):
        return pltpu.make_async_remote_copy(
            src_ref=src, dst_ref=dst, send_sem=send, recv_sem=recv, device_id=to, device_id_type=MESH
        )

    def in_copy(n, d):
        i = pl.ds(n * CI, CI)
        return copy(snd.at[i, xs[d]], rx.at[i, x], s1.at[n, d], r1.at[n, d], x_ids[d])

    def y_copy(n, d):
        i = pl.ds(n * CI, CI)
        t = xs[2 - d]
        return copy(rx.at[i, t, pl.ds(2, 2)], ry.at[i, t], s2.at[n, d], r2.at[n, d], y_id)

    def y_own(n):
        i = pl.ds(n * CI, CI)
        return copy(snd.at[i, x, pl.ds(2, 2)], ry.at[i, x], s2.at[n, 3], r2.at[n, 3], y_id)

    def back_copy(n):
        i = pl.ds(n * CI, CI)
        return copy(dkv.at[i, 1], ryd.at[i], s4.at[n], r4.at[n], y_id)

    def out_copy(n, d):
        i = pl.ds(n * CI, CI)
        return copy(outs.at[i, xs[d]], fin.at[i, x], s5.at[n, d], r5.at[n, d], x_ids[d])

    half = pl.ds(core * 512, 512)

    def bias_copy(d):
        return copy(bts.at[xs[d], half], btr.at[x, half], sb.at[d], rb.at[d], x_ids[d])

    def bias_twin(d):
        t = btr.at[xs[2 - d], half]
        return copy(t, t, sb.at[3 + d], rb.at[3 + d], core_id)

    def prepare(n):
        for one in range(CI):
            i = n * CI + one
            ga = do[i].astype(F32) * sigmoid(g[i].astype(F32))
            for t, array in enumerate((q[i], ga.astype(BF), k[i], v[i])):
                snd[i, :, t] = array.T.reshape(HEADS, C, 128)
            rx[i, x] = snd[i, x]

    def send_in(n):
        for d in range(3):
            in_copy(n, d).start()
        y_own(n).start()

    def forward(n, _):
        for d in range(3):
            in_copy(n, d).wait_recv()
            y_copy(n, d).start()
        return 0

    def forwarded(n):
        return jnp.minimum(chunks, 2 + n + lax.div(n, 3))

    for one_load in loads[:5]:
        one_load.wait()
    prepare(0)
    pl.semaphore_wait(barrier, len(everyone) + lax.rem(z + yl, 2))
    send_in(0)

    def bias_head(h, _):
        for p in range(2):
            for b in range(4):
                at = pl.multiple_of((2 * b + (yl if p == 0 else 1 - yl)) * 128, 128)
                bts[h, pl.ds((p * 4 + b) * 128, 128), :] = bias[h, :, pl.ds(at, 128)].T
        return 0

    loads[5].wait()
    lax.fori_loop(0, HEADS, bias_head, 0)
    for d in range(3):
        bias_copy(d).start()
    btr[x] = bts[x]

    def prepare_and_send(n, _):
        prepare(n)
        send_in(n)
        return 0

    for one_load in loads[6:]:
        one_load.wait()
    lax.fori_loop(1, chunks, prepare_and_send, 0)

    dacc[...] = jnp.zeros_like(dacc)
    forward(0, 0)
    for d in range(3):
        bias_copy(d).wait_recv()
        bias_twin(d).start()
    for d in range(3):
        bias_twin(d).wait_recv()
    valid = length[0]
    for p in range(2):
        for b in range(4):
            first = (2 * b + (yl if p == 0 else 1 - yl)) * 128
            ks = pl.ds((p * 4 + b) * 128, 128)
            live = lax.broadcasted_iota(jnp.int32, (128, 128), 0) + first < valid
            for t in range(4):
                bt[ks, pl.ds(t * 128, 128)] = jnp.where(live, btr[t, ks, :].astype(F32) * LOG2E, -1e30)

    def compute(n):
        def one(j, _):
            i = n * CI + j
            qt = jnp.concatenate([rx[i, t, 0] for t in range(4)], axis=1)
            gat = jnp.concatenate([rx[i, t, 1] for t in range(4)], axis=1)
            kt = jnp.concatenate([rx[i, t, 2] for t in range(4)] + [ry[i, t, 0] for t in range(4)], axis=1)
            vt = jnp.concatenate([rx[i, t, 3] for t in range(4)] + [ry[i, t, 1] for t in range(4)], axis=1)
            a, b, e, f = compute_row(qt, gat, kt, vt, bt, dacc, s_ref, e_ref, ds_ref, k2_ref, v1_ref)
            for t in range(4):
                js = slice(t * 128, t * 128 + 128)
                outs[i, t, 0] = a[:, js].astype(BF)
                outs[i, t, 1] = b[:, js].astype(BF)
                for p in range(2):
                    ks = slice((p * 4 + t) * 128, (p * 4 + t) * 128 + 128)
                    dkv[i, p, t, 0] = e[:, ks].astype(BF)
                    dkv[i, p, t, 1] = f[:, ks].astype(BF)
            return 0

        lax.fori_loop(0, CI, one, 0)

    def add_and_send(n):
        back_copy(n).wait_recv()
        for one in range(CI):
            i = n * CI + one
            total = dkv[i, 0].astype(F32) + ryd[i].astype(F32)
            outs[i, :, pl.ds(2, 2)] = total.astype(BF)
            fin[i, x] = outs[i, x]
        for d in range(3):
            out_copy(n, d).start()

    def finish(n):
        for d in range(3):
            out_copy(n, d).wait_recv()
        for one in range(CI):
            i = n * CI + one
            dq[i] = fin[i, :, 0].reshape(128, 128).T
            dk[i] = fin[i, :, 2].reshape(128, 128).T
            dv[i] = fin[i, :, 3].reshape(128, 128).T
            att = fin[i, :, 1].reshape(128, 128).T.astype(F32)
            s = sigmoid(g[i].astype(F32))
            dg[i] = (do[i].astype(F32) * att * s * (1.0 - s)).astype(BF)

    def finish_range(low, high):
        def one(n, _):
            finish(n)
            return 0

        lax.fori_loop(low, high, one, 0)

    def step(n, _):
        lax.fori_loop(forwarded(n), forwarded(n + 1), forward, 0)
        for d in range(3):
            y_copy(n, d).wait_recv()
        y_own(n).wait_recv()
        compute(n)
        back_copy(n).start()

        @pl.when(n >= ADD)
        def _():
            add_and_send(n - ADD)

        @pl.when(n >= LAG)
        def _():
            finish(n - LAG)

        return 0

    forward(1, 0)
    lax.fori_loop(0, chunks, step, 0)

    for t in range(4):
        for b in range(8):
            dt[pl.ds(t * 128, 128), pl.ds(b * 128, 128)] = dacc[pl.ds(b * 128, 128), pl.ds(t * 128, 128)].T
    for t in range(4):
        t1s[t] = dt[pl.ds(pl.multiple_of(t * 128 + 64 * (1 - core), 64), 64), :].astype(BF)
    one = copy(t1s, t1r, st.at[0], rt.at[0], core_id)
    one.start()
    add_and_send(chunks - 2)
    one.wait_recv()
    for t in range(4):
        total = dt[pl.ds(pl.multiple_of(t * 128 + 64 * core, 64), 64), :] + t1r[t].astype(F32)
        t2s[t, yl] = total[:, :512].astype(BF)
        t2s[t, 1 - yl] = total[:, 512:].astype(BF)
    me = yh * 4 + z
    three = []
    for d, (a, b) in enumerate(peers):
        src = t2s.at[2 * a + lax.div(b, 2), lax.rem(b, 2)]
        three.append(copy(src, t3r.at[me], st.at[1 + d], rt.at[1 + d], peer_ids[d]))
        three[-1].start()
    t3r[me] = t2s[2 * yh + lax.div(z, 2), lax.rem(z, 2)]
    finish_range(chunks - LAG, chunks - LAG + 2)
    add_and_send(chunks - 1)
    finish_range(chunks - LAG + 2, chunks - LAG + 5)
    for one_copy in three:
        one_copy.wait_recv()
    total = t3r[0].astype(F32)
    for s in range(1, 8):
        total += t3r[s].astype(F32)
    for t in range(4):
        t4s[t] = total[:, t * 128 : t * 128 + 128].astype(BF)
    four = []
    for d in range(3):
        four.append(copy(t4s.at[xs[d]], t4r.at[x], st.at[8 + d], rt.at[8 + d], last_ids[d]))
        four[-1].start()
    twin = copy(t4s.at[x], t4r.at[x], st.at[11], rt.at[11], twin_id)

    @pl.when(swaps)
    def _():
        twin.start()

    @pl.when(jnp.logical_not(swaps))
    def _():
        t4r[x] = t4s[x]

    finish_range(chunks - LAG + 5, chunks)
    for one_copy in four:
        one_copy.wait_recv()

    @pl.when(swaps)
    def _():
        twin.wait()

    for h in range(HEADS):
        db[h] = t4r[h].astype(F32)

    def drain(n, _):
        for d in range(3):
            in_copy(n, d).wait_send()
            out_copy(n, d).wait_send()
            y_copy(n, d).wait_send()
        y_own(n).wait_send()
        back_copy(n).wait_send()
        return 0

    lax.fori_loop(0, chunks, drain, 0)
    for d in range(3):
        bias_copy(d).wait_send()
        bias_twin(d).wait_send()
    for one_copy in [one] + three + four:
        one_copy.wait_send()


def store(*refs):
    sems = refs[-1]
    count = (len(refs) - 1) // 2
    copies = [pltpu.make_async_copy(refs[t], refs[count + t], sems.at[t]) for t in range(count)]
    for one in copies:
        one.start()
    for one in copies:
        one.wait()


def on_device(query, key, value, gate, d_out, bias, length):
    rows = query.shape[0]
    chunks = rows // CI
    vmem = pl.BlockSpec(memory_space=pltpu.VMEM)
    anywhere = pl.BlockSpec(memory_space=pl.ANY)
    pair = jax.ShapeDtypeStruct(query.shape, BF)
    dma = pltpu.SemaphoreType.DMA
    shapes = [pair, pair, pair, pair, jax.ShapeDtypeStruct((HEADS, 64, 128), F32)]
    out = pl.pallas_call(
        kernel,
        out_shape=[pltpu.VMEM(one.shape, one.dtype) for one in shapes],
        in_specs=[anywhere] * 6 + [pl.BlockSpec(memory_space=pltpu.SMEM)],
        out_specs=[vmem] * 5,
        scratch_shapes=[pltpu.VMEM(query.shape, BF)] * 5
        + [
            pltpu.VMEM(bias.shape, BF),
            dma((11,)),
            pltpu.VMEM((rows, 4, 4, C, 128), BF),
            pltpu.VMEM((rows, 4, 4, C, 128), BF),
            pltpu.VMEM((rows, 4, 2, C, 128), BF),
            pltpu.VMEM((rows, 2, 4, 2, C, 128), BF),
            pltpu.VMEM((rows, 4, 2, C, 128), BF),
            pltpu.VMEM((rows, 4, 4, C, 128), BF),
            pltpu.VMEM((rows, 4, 4, C, 128), BF),
            pltpu.VMEM((4, 1024, 128), BF),
            pltpu.VMEM((4, 1024, 128), BF),
            pltpu.VMEM((1024, 512), F32),
            pltpu.VMEM((1024, 512), F32),
            pltpu.VMEM((1024, 512), F32),
            pltpu.VMEM((1024, 512), BF),
            pltpu.VMEM((1024, 512), BF),
            pltpu.VMEM((1024, 64), BF),
            pltpu.VMEM((1024, 48), BF),
            pltpu.VMEM((512, 1024), F32),
            pltpu.VMEM((4, 64, 1024), BF),
            pltpu.VMEM((4, 64, 1024), BF),
            pltpu.VMEM((4, 2, 64, 512), BF),
            pltpu.VMEM((8, 64, 512), BF),
            pltpu.VMEM((4, 64, 128), BF),
            pltpu.VMEM((4, 64, 128), BF),
            dma((chunks, 3)), dma((chunks, 3)),
            dma((chunks, 4)), dma((chunks, 4)),
            dma((chunks,)), dma((chunks,)),
            dma((chunks, 3)), dma((chunks, 3)),
            dma((6,)), dma((6,)),
            dma((12,)), dma((12,)),
        ],
        compiler_params=pltpu.CompilerParams(
            collective_id=0, has_side_effects=True, vmem_limit_bytes=56 * 2**20
        ),
    )(query, key, value, gate, d_out, bias, length)
    out = pl.pallas_call(
        store,
        out_shape=shapes,
        in_specs=[vmem] * 5,
        out_specs=[anywhere] * 5,
        scratch_shapes=[dma((5,))],
        compiler_params=pltpu.CompilerParams(vmem_limit_bytes=6 * 2**20),
    )(*out)
    return tuple(out)


def solution(mesh):
    pair = P("row", "col", None)
    return jax.shard_map(
        on_device,
        mesh=mesh,
        in_specs=(pair,) * 5 + (P(None, "col", None), P()),
        out_specs=(pair,) * 4 + (P(None, "row", "col"),),
        check_vma=False,
    )
```

```python
import functools
import math

import jax
import jax.numpy as jnp
from jax import lax
from jax.experimental import pallas as pl
from jax.experimental.pallas import tpu as pltpu
from jax.sharding import PartitionSpec as P

MESH = pl.DeviceIdType.MESH
BF = jnp.bfloat16
F32 = jnp.float32
HEADS = 4
C = 32
SCALE = C**-0.5
LOG2E = math.log2(math.e)
CI = 2
LAG = 8
ADD = 2
KC = 256
NN = (((1,), (0,)), ((), ()))
NT = (((1,), (1,)), ((), ()))


def dot(a, b, dims=NN):
    return lax.dot_general(a, b, dims, preferred_element_type=F32)


def sigmoid(x):
    return 1.0 / (1.0 + jnp.exp(-x))


def compute_row(qt, gat, kt, vt, bt_ref, d_ref, s_ref, e_ref, ds_ref, k2_ref, v1_ref):
    n = kt.shape[1]
    width = qt.shape[1]
    k2_ref[...] = jnp.concatenate([kt, kt], axis=0).T
    v1t = jnp.concatenate([vt, jnp.ones((16, n), BF)], axis=0)
    v1_ref[...] = v1t.T
    row = lax.broadcasted_iota(jnp.int32, (16, width), 0)
    q = qt.astype(F32) * (SCALE * LOG2E)
    q_hi = q.astype(BF)
    q_lo = (q - q_hi.astype(F32)).astype(BF)
    q2 = jnp.concatenate([q_hi, q_lo], axis=0)
    peak = None
    for c in range(n // KC):
        ks = slice(c * KC, (c + 1) * KC)
        s = dot(k2_ref[ks, :], q2) + bt_ref[ks, :]
        s_ref[ks, :] = s
        part = jnp.max(s.reshape(KC // 8, 8, width), axis=0)
        peak = part if peak is None else jnp.maximum(peak, part)
    peak = jnp.max(peak, axis=0, keepdims=True)
    for c in range(n // KC):
        ks = slice(c * KC, (c + 1) * KC)
        e = jnp.exp2(s_ref[ks, :] - peak)
        s_ref[ks, :] = e
        e_ref[ks, :] = e.astype(BF)
    summed = dot(v1t, e_ref[...])
    inv = 1.0 / summed[C : C + 1, :]
    att = summed[:C, :] * inv
    ga = gat.astype(F32)
    row_dot = jnp.sum(ga * att, axis=0, keepdims=True) * inv
    ga_n = (ga * inv).astype(BF)
    r_hi = row_dot.astype(BF).astype(F32)
    r_lo = row_dot - r_hi
    ext = jnp.where(row == 0, -r_hi, jnp.where(row == 1, -r_lo, 0.0)).astype(BF)
    g1 = jnp.concatenate([ga_n, ext], axis=0)
    for c in range(n // KC):
        ks = slice(c * KC, (c + 1) * KC)
        ds = dot(v1_ref[ks, :], g1) * s_ref[ks, :]
        d_ref[ks, :] += ds
        ds_ref[ks, :] = ds.astype(BF)
    dq = dot(kt, ds_ref[...]) * SCALE
    dk = dot(qt, ds_ref[...], NT) * SCALE
    dv = dot(ga_n, e_ref[...], NT)
    return dq, att, dk, dv


def kernel(
    q_hbm, k_hbm, v_hbm, g_hbm, do_hbm, bias_hbm, length,
    dq, dk, dv, dg, db,
    q, k, v, g, do, bias, sl,
    snd, rx, ry, dkv, ryd, outs, fin,
    bts, btr, bt, dacc, s_ref, e_ref, ds_ref, k2_ref, v1_ref,
    dt, t1s, t1r, t2s, t3r, t4s, t4r,
    s1, r1, s2, r2, s4, r4, s5, r5, sb, rb, st, rt,
):
    loads = []
    for part, i in enumerate((pl.ds(0, CI), pl.ds(CI, q.shape[0] - CI))):
        for t, (far, near) in enumerate(((g_hbm, g), (do_hbm, do), (q_hbm, q), (k_hbm, k), (v_hbm, v))):
            loads.append(pltpu.make_async_copy(far.at[i], near.at[i], sl.at[part * 6 + t]))
        if part == 0:
            loads.append(pltpu.make_async_copy(bias_hbm, bias, sl.at[5]))
    for one_load in loads:
        one_load.start()

    r, c = lax.axis_index("row"), lax.axis_index("col")
    yh, z, core = lax.div(r, 8), lax.rem(lax.div(r, 2), 4), lax.rem(r, 2)
    x, yl = lax.div(c, 2), lax.rem(c, 2)
    rows = q.shape[0]
    chunks = rows // CI
    xs = [lax.rem(x + d, 4) for d in (1, 2, 3)]
    x_ids = [(r, t * 2 + yl) for t in xs]
    y_id = (r, x * 2 + 1 - yl)
    core_id = (r + 1 - 2 * core, c)
    peers = []
    for dyh in (0, 1):
        for dz in range(4):
            if dyh or dz:
                yh2 = yh if dyh == 0 else 1 - yh
                peers.append((yh2, lax.rem(z + dz, 4)))
    peer_ids = [(a * 8 + b * 2 + core, c) for a, b in peers]

    swap_row = yh * 8 + (lax.div(z, 2) * 2 + yl) * 2 + core
    swap_yl = lax.rem(z, 2)
    swaps = swap_yl != yl
    last_ids = [(swap_row, t * 2 + swap_yl) for t in xs]
    twin_id = (swap_row, x * 2 + swap_yl)

    everyone = x_ids + [y_id, core_id] + peer_ids + last_ids
    barrier = pltpu.get_barrier_semaphore()
    for one in everyone:
        pl.semaphore_signal(barrier, inc=1, device_id=one, device_id_type=MESH)

    @pl.when(swaps)
    def _():
        pl.semaphore_signal(barrier, inc=1, device_id=twin_id, device_id_type=MESH)

    def copy(src, dst, send, recv, to):
        return pltpu.make_async_remote_copy(
            src_ref=src, dst_ref=dst, send_sem=send, recv_sem=recv, device_id=to, device_id_type=MESH
        )

    def in_copy(n, d):
        i = pl.ds(n * CI, CI)
        return copy(snd.at[i, xs[d]], rx.at[i, x], s1.at[n, d], r1.at[n, d], x_ids[d])

    def y_copy(n, d):
        i = pl.ds(n * CI, CI)
        t = xs[2 - d]
        return copy(rx.at[i, t, pl.ds(2, 2)], ry.at[i, t], s2.at[n, d], r2.at[n, d], y_id)

    def y_own(n):
        i = pl.ds(n * CI, CI)
        return copy(snd.at[i, x, pl.ds(2, 2)], ry.at[i, x], s2.at[n, 3], r2.at[n, 3], y_id)

    def back_copy(n):
        i = pl.ds(n * CI, CI)
        return copy(dkv.at[i, 1], ryd.at[i], s4.at[n], r4.at[n], y_id)

    def out_copy(n, d):
        i = pl.ds(n * CI, CI)
        return copy(outs.at[i, xs[d]], fin.at[i, x], s5.at[n, d], r5.at[n, d], x_ids[d])

    half = pl.ds(core * 512, 512)

    def bias_copy(d):
        return copy(bts.at[xs[d], half], btr.at[x, half], sb.at[d], rb.at[d], x_ids[d])

    def bias_twin(d):
        t = btr.at[xs[2 - d], half]
        return copy(t, t, sb.at[3 + d], rb.at[3 + d], core_id)

    def prepare(n):
        for one in range(CI):
            i = n * CI + one
            ga = do[i].astype(F32) * sigmoid(g[i].astype(F32))
            for t, array in enumerate((q[i], ga.astype(BF), k[i], v[i])):
                snd[i, :, t] = array.T.reshape(HEADS, C, 128)
            rx[i, x] = snd[i, x]

    def send_in(n):
        for d in (1, 0, 2):
            in_copy(n, d).start()
        y_own(n).start()

    def forward(n, _):
        for d in range(3):
            in_copy(n, d).wait_recv()
            y_copy(n, d).start()
        return 0

    def forwarded(n):
        return jnp.minimum(chunks, 2 + n)

    for one_load in loads[:5]:
        one_load.wait()
    prepare(0)
    pl.semaphore_wait(barrier, len(everyone) + lax.rem(z + yl, 2))
    send_in(0)

    def bias_head(h, _):
        for p in range(2):
            for b in range(4):
                at = pl.multiple_of((2 * b + (yl if p == 0 else 1 - yl)) * 128, 128)
                bts[h, pl.ds((p * 4 + b) * 128, 128), :] = bias[h, :, pl.ds(at, 128)].T
        return 0

    loads[5].wait()
    lax.fori_loop(0, HEADS, bias_head, 0)
    for d in range(3):
        bias_copy(d).start()
    btr[x] = bts[x]

    def prepare_and_send(n, _):
        prepare(n)
        send_in(n)
        return 0

    for one_load in loads[6:]:
        one_load.wait()
    lax.fori_loop(1, chunks, prepare_and_send, 0)

    dacc[...] = jnp.zeros_like(dacc)
    forward(0, 0)
    for d in range(3):
        bias_copy(d).wait_recv()
        bias_twin(d).start()
    for d in range(3):
        bias_twin(d).wait_recv()
    valid = length[0]
    for p in range(2):
        for b in range(4):
            first = (2 * b + (yl if p == 0 else 1 - yl)) * 128
            ks = pl.ds((p * 4 + b) * 128, 128)
            live = lax.broadcasted_iota(jnp.int32, (128, 128), 0) + first < valid
            for t in range(4):
                bt[ks, pl.ds(t * 128, 128)] = jnp.where(live, btr[t, ks, :].astype(F32) * LOG2E, -1e30)

    def compute(n):
        def one(j, _):
            i = n * CI + j
            qt = jnp.concatenate([rx[i, t, 0] for t in range(4)], axis=1)
            gat = jnp.concatenate([rx[i, t, 1] for t in range(4)], axis=1)
            kt = jnp.concatenate([rx[i, t, 2] for t in range(4)] + [ry[i, t, 0] for t in range(4)], axis=1)
            vt = jnp.concatenate([rx[i, t, 3] for t in range(4)] + [ry[i, t, 1] for t in range(4)], axis=1)
            a, b, e, f = compute_row(qt, gat, kt, vt, bt, dacc, s_ref, e_ref, ds_ref, k2_ref, v1_ref)
            for t in range(4):
                js = slice(t * 128, t * 128 + 128)
                outs[i, t, 0] = a[:, js].astype(BF)
                outs[i, t, 1] = b[:, js].astype(BF)
                for p in range(2):
                    ks = slice((p * 4 + t) * 128, (p * 4 + t) * 128 + 128)
                    dkv[i, p, t, 0] = e[:, ks].astype(BF)
                    dkv[i, p, t, 1] = f[:, ks].astype(BF)
            return 0

        lax.fori_loop(0, CI, one, 0)

    def add_and_send(n):
        back_copy(n).wait_recv()
        for one in range(CI):
            i = n * CI + one
            total = dkv[i, 0].astype(F32) + ryd[i].astype(F32)
            outs[i, :, pl.ds(2, 2)] = total.astype(BF)
            fin[i, x] = outs[i, x]
        for d in range(3):
            out_copy(n, d).start()

    def finish(n):
        for d in range(3):
            out_copy(n, d).wait_recv()
        for one in range(CI):
            i = n * CI + one
            dq[i] = fin[i, :, 0].reshape(128, 128).T
            dk[i] = fin[i, :, 2].reshape(128, 128).T
            dv[i] = fin[i, :, 3].reshape(128, 128).T
            att = fin[i, :, 1].reshape(128, 128).T.astype(F32)
            s = sigmoid(g[i].astype(F32))
            dg[i] = (do[i].astype(F32) * att * s * (1.0 - s)).astype(BF)

    def finish_range(low, high):
        def one(n, _):
            finish(n)
            return 0

        lax.fori_loop(low, high, one, 0)

    def step(n, _):
        lax.fori_loop(forwarded(n), forwarded(n + 1), forward, 0)
        for d in range(3):
            y_copy(n, d).wait_recv()
        y_own(n).wait_recv()
        compute(n)
        back_copy(n).start()

        @pl.when(n >= ADD)
        def _():
            add_and_send(n - ADD)

        @pl.when(n >= LAG)
        def _():
            finish(n - LAG)

        return 0

    forward(1, 0)
    lax.fori_loop(0, chunks, step, 0)

    for t in range(4):
        for b in range(8):
            dt[pl.ds(t * 128, 128), pl.ds(b * 128, 128)] = dacc[pl.ds(b * 128, 128), pl.ds(t * 128, 128)].T
    for t in range(4):
        t1s[t] = dt[pl.ds(pl.multiple_of(t * 128 + 64 * (1 - core), 64), 64), :].astype(BF)
    one = copy(t1s, t1r, st.at[0], rt.at[0], core_id)
    one.start()
    one.wait_recv()
    for t in range(4):
        total = dt[pl.ds(pl.multiple_of(t * 128 + 64 * core, 64), 64), :] + t1r[t].astype(F32)
        t2s[t, yl] = total[:, :512].astype(BF)
        t2s[t, 1 - yl] = total[:, 512:].astype(BF)
    me = yh * 4 + z
    three = []
    for d, (a, b) in enumerate(peers):
        src = t2s.at[2 * a + lax.div(b, 2), lax.rem(b, 2)]
        three.append(copy(src, t3r.at[me], st.at[1 + d], rt.at[1 + d], peer_ids[d]))
        three[-1].start()
    t3r[me] = t2s[2 * yh + lax.div(z, 2), lax.rem(z, 2)]
    add_and_send(chunks - 2)
    add_and_send(chunks - 1)
    finish_range(chunks - LAG, chunks - LAG + 5)
    for one_copy in three:
        one_copy.wait_recv()
    total = t3r[0].astype(F32)
    for s in range(1, 8):
        total += t3r[s].astype(F32)
    for t in range(4):
        t4s[t] = total[:, t * 128 : t * 128 + 128].astype(BF)
    four = []
    for d in range(3):
        four.append(copy(t4s.at[xs[d]], t4r.at[x], st.at[8 + d], rt.at[8 + d], last_ids[d]))
        four[-1].start()
    twin = copy(t4s.at[x], t4r.at[x], st.at[11], rt.at[11], twin_id)

    @pl.when(swaps)
    def _():
        twin.start()

    @pl.when(jnp.logical_not(swaps))
    def _():
        t4r[x] = t4s[x]

    finish_range(chunks - LAG + 5, chunks)
    for one_copy in four:
        one_copy.wait_recv()

    @pl.when(swaps)
    def _():
        twin.wait()

    for h in range(HEADS):
        db[h] = t4r[h].astype(F32)

    def drain(n, _):
        for d in range(3):
            in_copy(n, d).wait_send()
            out_copy(n, d).wait_send()
            y_copy(n, d).wait_send()
        y_own(n).wait_send()
        back_copy(n).wait_send()
        return 0

    lax.fori_loop(0, chunks, drain, 0)
    for d in range(3):
        bias_copy(d).wait_send()
        bias_twin(d).wait_send()
    for one_copy in [one] + three + four:
        one_copy.wait_send()


def store(*refs):
    sems = refs[-1]
    count = (len(refs) - 1) // 2
    copies = [pltpu.make_async_copy(refs[t], refs[count + t], sems.at[t]) for t in range(count)]
    for one in copies:
        one.start()
    for one in copies:
        one.wait()


def on_device(query, key, value, gate, d_out, bias, length):
    rows = query.shape[0]
    chunks = rows // CI
    vmem = pl.BlockSpec(memory_space=pltpu.VMEM)
    anywhere = pl.BlockSpec(memory_space=pl.ANY)
    pair = jax.ShapeDtypeStruct(query.shape, BF)
    dma = pltpu.SemaphoreType.DMA
    shapes = [pair, pair, pair, pair, jax.ShapeDtypeStruct((HEADS, 64, 128), F32)]
    out = pl.pallas_call(
        kernel,
        out_shape=[pltpu.VMEM(one.shape, one.dtype) for one in shapes],
        in_specs=[anywhere] * 6 + [pl.BlockSpec(memory_space=pltpu.SMEM)],
        out_specs=[vmem] * 5,
        scratch_shapes=[pltpu.VMEM(query.shape, BF)] * 5
        + [
            pltpu.VMEM(bias.shape, BF),
            dma((11,)),
            pltpu.VMEM((rows, 4, 4, C, 128), BF),
            pltpu.VMEM((rows, 4, 4, C, 128), BF),
            pltpu.VMEM((rows, 4, 2, C, 128), BF),
            pltpu.VMEM((rows, 2, 4, 2, C, 128), BF),
            pltpu.VMEM((rows, 4, 2, C, 128), BF),
            pltpu.VMEM((rows, 4, 4, C, 128), BF),
            pltpu.VMEM((rows, 4, 4, C, 128), BF),
            pltpu.VMEM((4, 1024, 128), BF),
            pltpu.VMEM((4, 1024, 128), BF),
            pltpu.VMEM((1024, 512), F32),
            pltpu.VMEM((1024, 512), F32),
            pltpu.VMEM((1024, 512), F32),
            pltpu.VMEM((1024, 512), BF),
            pltpu.VMEM((1024, 512), BF),
            pltpu.VMEM((1024, 64), BF),
            pltpu.VMEM((1024, 48), BF),
            pltpu.VMEM((512, 1024), F32),
            pltpu.VMEM((4, 64, 1024), BF),
            pltpu.VMEM((4, 64, 1024), BF),
            pltpu.VMEM((4, 2, 64, 512), BF),
            pltpu.VMEM((8, 64, 512), BF),
            pltpu.VMEM((4, 64, 128), BF),
            pltpu.VMEM((4, 64, 128), BF),
            dma((chunks, 3)), dma((chunks, 3)),
            dma((chunks, 4)), dma((chunks, 4)),
            dma((chunks,)), dma((chunks,)),
            dma((chunks, 3)), dma((chunks, 3)),
            dma((6,)), dma((6,)),
            dma((12,)), dma((12,)),
        ],
        compiler_params=pltpu.CompilerParams(
            collective_id=0, has_side_effects=True, vmem_limit_bytes=56 * 2**20
        ),
    )(query, key, value, gate, d_out, bias, length)
    out = pl.pallas_call(
        store,
        out_shape=shapes,
        in_specs=[vmem] * 5,
        out_specs=[anywhere] * 5,
        scratch_shapes=[dma((5,))],
        compiler_params=pltpu.CompilerParams(vmem_limit_bytes=6 * 2**20),
    )(*out)
    return tuple(out)


def solution(mesh):
    pair = P("row", "col", None)
    return jax.shard_map(
        on_device,
        mesh=mesh,
        in_specs=(pair,) * 5 + (P(None, "col", None), P()),
        out_specs=(pair,) * 4 + (P(None, "row", "col"),),
        check_vma=False,
    )
```

```python
import functools
import math

import jax
import jax.numpy as jnp
from jax import lax
from jax.experimental import pallas as pl
from jax.experimental.pallas import tpu as pltpu
from jax.sharding import PartitionSpec as P

MESH = pl.DeviceIdType.MESH
BF = jnp.bfloat16
F32 = jnp.float32
HEADS = 4
C = 32
SCALE = C**-0.5
LOG2E = math.log2(math.e)
CI = 2
LAG = 6
ADD = 2
KC = 256
NN = (((1,), (0,)), ((), ()))
NT = (((1,), (1,)), ((), ()))


def dot(a, b, dims=NN):
    return lax.dot_general(a, b, dims, preferred_element_type=F32)


def sigmoid(x):
    return 1.0 / (1.0 + jnp.exp(-x))


def compute_row(qt, gat, kt, vt, bt_ref, d_ref, s_ref, e_ref, ds_ref, k2_ref, v1_ref):
    n = kt.shape[1]
    width = qt.shape[1]
    k2_ref[...] = jnp.concatenate([kt, kt], axis=0).T
    v1t = jnp.concatenate([vt, jnp.ones((16, n), BF)], axis=0)
    v1_ref[...] = v1t.T
    row = lax.broadcasted_iota(jnp.int32, (16, width), 0)
    q = qt.astype(F32) * (SCALE * LOG2E)
    q_hi = q.astype(BF)
    q_lo = (q - q_hi.astype(F32)).astype(BF)
    q2 = jnp.concatenate([q_hi, q_lo], axis=0)
    peak = None
    for c in range(n // KC):
        ks = slice(c * KC, (c + 1) * KC)
        s = dot(k2_ref[ks, :], q2) + bt_ref[ks, :]
        s_ref[ks, :] = s
        part = jnp.max(s.reshape(KC // 8, 8, width), axis=0)
        peak = part if peak is None else jnp.maximum(peak, part)
    peak = jnp.max(peak, axis=0, keepdims=True)
    for c in range(n // KC):
        ks = slice(c * KC, (c + 1) * KC)
        e = jnp.exp2(s_ref[ks, :] - peak)
        s_ref[ks, :] = e
        e_ref[ks, :] = e.astype(BF)
    summed = dot(v1t, e_ref[...])
    inv = 1.0 / summed[C : C + 1, :]
    att = summed[:C, :] * inv
    ga = gat.astype(F32)
    row_dot = jnp.sum(ga * att, axis=0, keepdims=True) * inv
    ga_n = (ga * inv).astype(BF)
    r_hi = row_dot.astype(BF).astype(F32)
    r_lo = row_dot - r_hi
    ext = jnp.where(row == 0, -r_hi, jnp.where(row == 1, -r_lo, 0.0)).astype(BF)
    g1 = jnp.concatenate([ga_n, ext], axis=0)
    for c in range(n // KC):
        ks = slice(c * KC, (c + 1) * KC)
        ds = dot(v1_ref[ks, :], g1) * s_ref[ks, :]
        d_ref[ks, :] += ds
        ds_ref[ks, :] = ds.astype(BF)
    dq = dot(kt, ds_ref[...]) * SCALE
    dk = dot(qt, ds_ref[...], NT) * SCALE
    dv = dot(ga_n, e_ref[...], NT)
    return dq, att, dk, dv


def kernel(
    q_hbm, k_hbm, v_hbm, g_hbm, do_hbm, bias_hbm, length,
    dq, dk, dv, dg, db,
    q, k, v, g, do, bias, sl,
    snd, rx, ry, dkv, ryd, outs, fin,
    bts, btr, bt, dacc, s_ref, e_ref, ds_ref, k2_ref, v1_ref,
    dt, t1s, t1r, t2s, t3r, t4s, t4r,
    s1, r1, s2, r2, s4, r4, s5, r5, sb, rb, st, rt,
):
    loads = []
    for part, i in enumerate((pl.ds(0, CI), pl.ds(CI, q.shape[0] - CI))):
        for t, (far, near) in enumerate(((g_hbm, g), (do_hbm, do), (q_hbm, q), (k_hbm, k), (v_hbm, v))):
            loads.append(pltpu.make_async_copy(far.at[i], near.at[i], sl.at[part * 6 + t]))
        if part == 0:
            loads.append(pltpu.make_async_copy(bias_hbm, bias, sl.at[5]))
    for one_load in loads:
        one_load.start()

    r, c = lax.axis_index("row"), lax.axis_index("col")
    yh, z, core = lax.div(r, 8), lax.rem(lax.div(r, 2), 4), lax.rem(r, 2)
    x, yl = lax.div(c, 2), lax.rem(c, 2)
    rows = q.shape[0]
    chunks = rows // CI
    xs = [lax.rem(x + d, 4) for d in (1, 2, 3)]
    x_ids = [(r, t * 2 + yl) for t in xs]
    y_id = (r, x * 2 + 1 - yl)
    core_id = (r + 1 - 2 * core, c)
    peers = []
    for dyh in (0, 1):
        for dz in range(4):
            if dyh or dz:
                yh2 = yh if dyh == 0 else 1 - yh
                peers.append((yh2, lax.rem(z + dz, 4)))
    peer_ids = [(a * 8 + b * 2 + core, c) for a, b in peers]

    swap_row = yh * 8 + (lax.div(z, 2) * 2 + yl) * 2 + core
    swap_yl = lax.rem(z, 2)
    swaps = swap_yl != yl
    last_ids = [(swap_row, t * 2 + swap_yl) for t in xs]
    twin_id = (swap_row, x * 2 + swap_yl)

    everyone = x_ids + [y_id, core_id] + peer_ids + last_ids
    barrier = pltpu.get_barrier_semaphore()
    for one in everyone:
        pl.semaphore_signal(barrier, inc=1, device_id=one, device_id_type=MESH)

    @pl.when(swaps)
    def _():
        pl.semaphore_signal(barrier, inc=1, device_id=twin_id, device_id_type=MESH)

    def copy(src, dst, send, recv, to):
        return pltpu.make_async_remote_copy(
            src_ref=src, dst_ref=dst, send_sem=send, recv_sem=recv, device_id=to, device_id_type=MESH
        )

    def in_copy(n, d):
        i = pl.ds(n * CI, CI)
        return copy(snd.at[i, xs[d]], rx.at[i, x], s1.at[n, d], r1.at[n, d], x_ids[d])

    def y_copy(n, d):
        i = pl.ds(n * CI, CI)
        t = xs[2 - d]
        return copy(rx.at[i, t, pl.ds(2, 2)], ry.at[i, t], s2.at[n, d], r2.at[n, d], y_id)

    def y_own(n):
        i = pl.ds(n * CI, CI)
        return copy(snd.at[i, x, pl.ds(2, 2)], ry.at[i, x], s2.at[n, 3], r2.at[n, 3], y_id)

    def back_copy(n):
        i = pl.ds(n * CI, CI)
        return copy(dkv.at[i, 1], ryd.at[i], s4.at[n], r4.at[n], y_id)

    def out_copy(n, d):
        i = pl.ds(n * CI, CI)
        return copy(outs.at[i, xs[d]], fin.at[i, x], s5.at[n, d], r5.at[n, d], x_ids[d])

    half = pl.ds(core * 512, 512)

    def bias_copy(d):
        return copy(bts.at[xs[d], half], btr.at[x, half], sb.at[d], rb.at[d], x_ids[d])

    def bias_twin(d):
        t = btr.at[xs[2 - d], half]
        return copy(t, t, sb.at[3 + d], rb.at[3 + d], core_id)

    def prepare(n):
        for one in range(CI):
            i = n * CI + one
            ga = do[i].astype(F32) * sigmoid(g[i].astype(F32))
            for t, array in enumerate((q[i], ga.astype(BF), k[i], v[i])):
                snd[i, :, t] = array.T.reshape(HEADS, C, 128)
            rx[i, x] = snd[i, x]

    def send_in(n):
        for d in (1, 0, 2):
            in_copy(n, d).start()
        y_own(n).start()

    def forward(n, _):
        for d in range(3):
            in_copy(n, d).wait_recv()
            y_copy(n, d).start()
        return 0

    def forwarded(n):
        return jnp.minimum(chunks, 2 + n)

    for one_load in loads[:5]:
        one_load.wait()
    prepare(0)
    pl.semaphore_wait(barrier, len(everyone) + lax.rem(z + yl, 2))
    send_in(0)

    def bias_head(h, _):
        for p in range(2):
            for b in range(4):
                at = pl.multiple_of((2 * b + (yl if p == 0 else 1 - yl)) * 128, 128)
                bts[h, pl.ds((p * 4 + b) * 128, 128), :] = bias[h, :, pl.ds(at, 128)].T
        return 0

    loads[5].wait()
    lax.fori_loop(0, HEADS, bias_head, 0)
    for d in range(3):
        bias_copy(d).start()
    btr[x] = bts[x]

    def prepare_and_send(n, _):
        prepare(n)
        send_in(n)
        return 0

    for one_load in loads[6:]:
        one_load.wait()
    lax.fori_loop(1, chunks, prepare_and_send, 0)

    dacc[...] = jnp.zeros_like(dacc)
    forward(0, 0)
    for d in range(3):
        bias_copy(d).wait_recv()
        bias_twin(d).start()
    for d in range(3):
        bias_twin(d).wait_recv()
    valid = length[0]
    for p in range(2):
        for b in range(4):
            first = (2 * b + (yl if p == 0 else 1 - yl)) * 128
            ks = pl.ds((p * 4 + b) * 128, 128)
            live = lax.broadcasted_iota(jnp.int32, (128, 128), 0) + first < valid
            for t in range(4):
                bt[ks, pl.ds(t * 128, 128)] = jnp.where(live, btr[t, ks, :].astype(F32) * LOG2E, -1e30)

    def compute(n):
        def one(j, _):
            i = n * CI + j
            qt = jnp.concatenate([rx[i, t, 0] for t in range(4)], axis=1)
            gat = jnp.concatenate([rx[i, t, 1] for t in range(4)], axis=1)
            kt = jnp.concatenate([rx[i, t, 2] for t in range(4)] + [ry[i, t, 0] for t in range(4)], axis=1)
            vt = jnp.concatenate([rx[i, t, 3] for t in range(4)] + [ry[i, t, 1] for t in range(4)], axis=1)
            a, b, e, f = compute_row(qt, gat, kt, vt, bt, dacc, s_ref, e_ref, ds_ref, k2_ref, v1_ref)
            for t in range(4):
                js = slice(t * 128, t * 128 + 128)
                outs[i, t, 0] = a[:, js].astype(BF)
                outs[i, t, 1] = b[:, js].astype(BF)
                for p in range(2):
                    ks = slice((p * 4 + t) * 128, (p * 4 + t) * 128 + 128)
                    dkv[i, p, t, 0] = e[:, ks].astype(BF)
                    dkv[i, p, t, 1] = f[:, ks].astype(BF)
            return 0

        lax.fori_loop(0, CI, one, 0)

    def add_and_send(n):
        back_copy(n).wait_recv()
        for one in range(CI):
            i = n * CI + one
            total = dkv[i, 0].astype(F32) + ryd[i].astype(F32)
            outs[i, :, pl.ds(2, 2)] = total.astype(BF)
            fin[i, x] = outs[i, x]
        for d in range(3):
            out_copy(n, d).start()

    def finish(n):
        for d in range(3):
            out_copy(n, d).wait_recv()
        for one in range(CI):
            i = n * CI + one
            dq[i] = fin[i, :, 0].reshape(128, 128).T
            dk[i] = fin[i, :, 2].reshape(128, 128).T
            dv[i] = fin[i, :, 3].reshape(128, 128).T
            att = fin[i, :, 1].reshape(128, 128).T.astype(F32)
            s = sigmoid(g[i].astype(F32))
            dg[i] = (do[i].astype(F32) * att * s * (1.0 - s)).astype(BF)

    def finish_range(low, high):
        def one(n, _):
            finish(n)
            return 0

        lax.fori_loop(low, high, one, 0)

    def step(n, _):
        lax.fori_loop(forwarded(n), forwarded(n + 1), forward, 0)
        for d in range(3):
            y_copy(n, d).wait_recv()
        y_own(n).wait_recv()
        compute(n)
        back_copy(n).start()

        @pl.when(n >= ADD)
        def _():
            add_and_send(n - ADD)

        @pl.when(n >= LAG)
        def _():
            finish(n - LAG)

        return 0

    forward(1, 0)
    lax.fori_loop(0, chunks, step, 0)

    for t in range(4):
        for b in range(8):
            dt[pl.ds(t * 128, 128), pl.ds(b * 128, 128)] = dacc[pl.ds(b * 128, 128), pl.ds(t * 128, 128)].T
    for t in range(4):
        t1s[t] = dt[pl.ds(pl.multiple_of(t * 128 + 64 * (1 - core), 64), 64), :].astype(BF)
    one = copy(t1s, t1r, st.at[0], rt.at[0], core_id)
    one.start()
    one.wait_recv()
    for t in range(4):
        total = dt[pl.ds(pl.multiple_of(t * 128 + 64 * core, 64), 64), :] + t1r[t].astype(F32)
        t2s[t, yl] = total[:, :512].astype(BF)
        t2s[t, 1 - yl] = total[:, 512:].astype(BF)
    me = yh * 4 + z
    three = []
    for d, (a, b) in enumerate(peers):
        src = t2s.at[2 * a + lax.div(b, 2), lax.rem(b, 2)]
        three.append(copy(src, t3r.at[me], st.at[1 + d], rt.at[1 + d], peer_ids[d]))
        three[-1].start()
    t3r[me] = t2s[2 * yh + lax.div(z, 2), lax.rem(z, 2)]
    add_and_send(chunks - 2)
    add_and_send(chunks - 1)
    finish_range(chunks - LAG, chunks - LAG + 5)
    for one_copy in three:
        one_copy.wait_recv()
    total = t3r[0].astype(F32)
    for s in range(1, 8):
        total += t3r[s].astype(F32)
    for t in range(4):
        t4s[t] = total[:, t * 128 : t * 128 + 128].astype(BF)
    four = []
    for d in range(3):
        four.append(copy(t4s.at[xs[d]], t4r.at[x], st.at[8 + d], rt.at[8 + d], last_ids[d]))
        four[-1].start()
    twin = copy(t4s.at[x], t4r.at[x], st.at[11], rt.at[11], twin_id)

    @pl.when(swaps)
    def _():
        twin.start()

    @pl.when(jnp.logical_not(swaps))
    def _():
        t4r[x] = t4s[x]

    finish_range(chunks - LAG + 5, chunks)
    for one_copy in four:
        one_copy.wait_recv()

    @pl.when(swaps)
    def _():
        twin.wait()

    for h in range(HEADS):
        db[h] = t4r[h].astype(F32)

    def drain(n, _):
        for d in range(3):
            in_copy(n, d).wait_send()
            out_copy(n, d).wait_send()
            y_copy(n, d).wait_send()
        y_own(n).wait_send()
        back_copy(n).wait_send()
        return 0

    lax.fori_loop(0, chunks, drain, 0)
    for d in range(3):
        bias_copy(d).wait_send()
        bias_twin(d).wait_send()
    for one_copy in [one] + three + four:
        one_copy.wait_send()


def store(*refs):
    sems = refs[-1]
    count = (len(refs) - 1) // 2
    copies = [pltpu.make_async_copy(refs[t], refs[count + t], sems.at[t]) for t in range(count)]
    for one in copies:
        one.start()
    for one in copies:
        one.wait()


def on_device(query, key, value, gate, d_out, bias, length):
    rows = query.shape[0]
    chunks = rows // CI
    vmem = pl.BlockSpec(memory_space=pltpu.VMEM)
    anywhere = pl.BlockSpec(memory_space=pl.ANY)
    pair = jax.ShapeDtypeStruct(query.shape, BF)
    dma = pltpu.SemaphoreType.DMA
    shapes = [pair, pair, pair, pair, jax.ShapeDtypeStruct((HEADS, 64, 128), F32)]
    out = pl.pallas_call(
        kernel,
        out_shape=[pltpu.VMEM(one.shape, one.dtype) for one in shapes],
        in_specs=[anywhere] * 6 + [pl.BlockSpec(memory_space=pltpu.SMEM)],
        out_specs=[vmem] * 5,
        scratch_shapes=[pltpu.VMEM(query.shape, BF)] * 5
        + [
            pltpu.VMEM(bias.shape, BF),
            dma((11,)),
            pltpu.VMEM((rows, 4, 4, C, 128), BF),
            pltpu.VMEM((rows, 4, 4, C, 128), BF),
            pltpu.VMEM((rows, 4, 2, C, 128), BF),
            pltpu.VMEM((rows, 2, 4, 2, C, 128), BF),
            pltpu.VMEM((rows, 4, 2, C, 128), BF),
            pltpu.VMEM((rows, 4, 4, C, 128), BF),
            pltpu.VMEM((rows, 4, 4, C, 128), BF),
            pltpu.VMEM((4, 1024, 128), BF),
            pltpu.VMEM((4, 1024, 128), BF),
            pltpu.VMEM((1024, 512), F32),
            pltpu.VMEM((1024, 512), F32),
            pltpu.VMEM((1024, 512), F32),
            pltpu.VMEM((1024, 512), BF),
            pltpu.VMEM((1024, 512), BF),
            pltpu.VMEM((1024, 64), BF),
            pltpu.VMEM((1024, 48), BF),
            pltpu.VMEM((512, 1024), F32),
            pltpu.VMEM((4, 64, 1024), BF),
            pltpu.VMEM((4, 64, 1024), BF),
            pltpu.VMEM((4, 2, 64, 512), BF),
            pltpu.VMEM((8, 64, 512), BF),
            pltpu.VMEM((4, 64, 128), BF),
            pltpu.VMEM((4, 64, 128), BF),
            dma((chunks, 3)), dma((chunks, 3)),
            dma((chunks, 4)), dma((chunks, 4)),
            dma((chunks,)), dma((chunks,)),
            dma((chunks, 3)), dma((chunks, 3)),
            dma((6,)), dma((6,)),
            dma((12,)), dma((12,)),
        ],
        compiler_params=pltpu.CompilerParams(
            collective_id=0, has_side_effects=True, vmem_limit_bytes=56 * 2**20
        ),
    )(query, key, value, gate, d_out, bias, length)
    out = pl.pallas_call(
        store,
        out_shape=shapes,
        in_specs=[vmem] * 5,
        out_specs=[anywhere] * 5,
        scratch_shapes=[dma((5,))],
        compiler_params=pltpu.CompilerParams(vmem_limit_bytes=6 * 2**20),
    )(*out)
    return tuple(out)


def solution(mesh):
    pair = P("row", "col", None)
    return jax.shard_map(
        on_device,
        mesh=mesh,
        in_specs=(pair,) * 5 + (P(None, "col", None), P()),
        out_specs=(pair,) * 4 + (P(None, "row", "col"),),
        check_vma=False,
    )
```
